32 devices in a mesh: rep: 8 (over y, x, core), shard: 4 (over z).
Axes of the slice: x: 2, y: 2, z: 4, core: 2. Of those that a mesh axis runs over, the one named last changes fastest.
Arguments:
- tokens: bfloat16 [4096, 2048], P(('rep', 'shard')), may hold values from -6 to 6
- lengths: int32 [32], P(('rep', 'shard')), may hold values from 1 to 128, 3072 in all
- norm1_gain: float32 [2048], replicated, may hold values from 0.5 to 1.5
- norm1_bias: float32 [2048], replicated, may hold values from -3 to 3
- w_qkv: bfloat16 [8, 768, 2048], P(None, 'shard'), may hold values from -0.125 to 0.125
- b_qkv: float32 [6144], replicated, may hold values from -3 to 3
- w_out: bfloat16 [8, 256, 2048], P(None, 'shard'), may hold values from -1 to 1
- norm2_gain: float32 [2048], replicated, may hold values from 0.5 to 1.5
- norm2_bias: float32 [2048], replicated, may hold values from -3 to 3
- w_gate_up: bfloat16 [8, 1408, 2048], P(None, 'shard'), may hold values from -0.125 to 0.125
- w_down: bfloat16 [8, 256, 5632], P(None, 'shard'), may hold values from -0.15625 to 0.15625
- cotangent: bfloat16 [4096, 2048], P(('rep', 'shard')), may hold values from -6 to 6
Outputs:
- mixed: float32 [4096, 2048], P(('rep', 'shard'))
- grad_tokens: float32 [4096, 2048], P(('rep', 'shard'))
- grad_norm1_gain: float32 [2048], replicated
- grad_norm1_bias: float32 [2048], replicated
- grad_w_qkv: float32 [8, 768, 2048], P(None, 'shard')
- grad_b_qkv: float32 [6144], replicated
- grad_w_out: float32 [8, 256, 2048], P(None, 'shard')
- grad_norm2_gain: float32 [2048], replicated
- grad_norm2_bias: float32 [2048], replicated
- grad_w_gate_up: float32 [8, 1408, 2048], P(None, 'shard')
- grad_w_down: float32 [8, 256, 5632], P(None, 'shard')
The draws below stay inside these ranges and needn't reach their ends.
Inputs may be any that keep to these rules, and one draw needn't show every extreme that they name: The lengths sum to 3072 and the longest is 128.
All inputs are finite; a program needn't handle non-finite values. No bound on the sum of `lengths` on one device may be relied on, other than what follows from the above.
Results may differ from the reference program's by a relative error of at most 0.017.
Values may be sent and summed in bfloat16 or wider, within the bound.
No kernel may reach another device: no remote copies, remote signals or barrier semaphores. Data moves between devices by JAX's collectives and lax.ppermute only.
A program may use at most 320 MiB of HBM per device.

```python
import math
import jax
import jax.numpy as jnp
import numpy as np
from jax import lax

D = 2048
HEAD = 64
FF = 5632
ROT = 16
LEN = 128
SEQS = 32
TOKENS = 4096
N_REP = 8


def strengthened(values, stream_key, source, target, parts, factor):
    def block_of(axis_at):
        return (jnp.arange(values.shape[axis_at]) // (values.shape[axis_at] // parts)).reshape((-1,) + (1,) * (values.ndim - 1 - axis_at))

    one_side = jax.random.permutation(stream_key, parts)[block_of(target)]
    second = (block_of(target) + parts // 2) % parts
    return jnp.where((block_of(source) == one_side) | (block_of(source) == second), factor * values, values)


def level_of(stream_key, extent, cuts, least, largest):
    level, own = 1.0, jax.random.fold_in(stream_key, 6)
    for axis_at, blocks in cuts:
        steps = jnp.exp(jax.random.uniform(jax.random.fold_in(own, axis_at), (blocks,), jnp.float32, least / len(cuts), largest / len(cuts)))
        level = level * jnp.repeat(steps, extent[axis_at] // blocks).reshape([-1 if axis == axis_at else 1 for axis in range(len(extent))])
    return level


def length_profile(count, total, limit, slope):
    portions = [(1 << 20) // math.isqrt(grade ** slope) + 1 for grade in range(2, count + 1)]
    rest, holding = total - limit - (count - 1), [1] * (count - 1)
    while rest > 0:
        free = [i for i in range(count - 1) if holding[i] < limit]
        whole, budget = sum([portions[i] for i in free]), rest
        for i in free:
            extra = min(limit - holding[i], max(1, budget * portions[i] // whole), rest)
            holding[i] = holding[i] + extra
            rest = rest - extra
    return np.array([limit] + holding)


def ragged(key, count, total, limit, lean):
    if count == 2:
        one = jax.random.randint(key, (), max(1, total - limit), min(limit, total - 1) + 1)
        return jnp.stack([one, total - one])
    sizes = jnp.asarray(length_profile(count, total, limit, lean), jnp.int32)
    couples = (count - 1) // 2
    source_of, receiver = sizes[1:1 + 2 * couples:2], sizes[2:2 + 2 * couples:2]
    slack = jnp.minimum(source_of - 1, limit - receiver)
    moved = jax.random.randint(jax.random.fold_in(key, 1), (couples,), 0, 1 << 20) % (slack + 1)
    sizes = sizes.at[1:1 + 2 * couples:2].set(source_of - moved).at[2:2 + 2 * couples:2].set(receiver + moved)
    return sizes[jax.random.permutation(jax.random.fold_in(key, 2), count)]


def scatter_about(own_key, dims, scale, bound, split=(), held_as=jnp.bfloat16):
    entries = jax.random.normal(own_key, dims, jnp.float32) * scale
    if len(split) > 0:
        entries = level_of(own_key, dims, split, -0.22, 0.18) * entries
    return jnp.clip(entries, min=-bound, max=bound).astype(held_as)


def bell_draw_with(rng, shape, scale, bound, shards, heavy, kind=jnp.bfloat16):
    values = scale * jax.random.normal(rng, shape, jnp.float32)
    if shards:
        values = values * level_of(rng, shape, shards, -0.22, 0.18)
    return jnp.clip(strengthened(values, jax.random.fold_in(rng, 3), *heavy), -bound, bound).astype(kind)


def setup_inputs(seed: int = 0) -> dict:
    key_list = jax.random.split(jax.random.key(seed), 13)
    tokens = scatter_about(key_list[0], (TOKENS, D), 1.0, 6.0, ((0, 32),))
    lengths = ragged(key_list[1], SEQS, TOKENS * 3 // 4, LEN, 1).astype(jnp.int32)
    norm1_gain = jnp.clip(1.0 + 0.1 * jax.random.normal(key_list[2], (D,), jnp.float32), 0.5, 1.5)
    norm1_bias = scatter_about(key_list[3], (D,), 0.3, 3.0, (), jnp.float32)
    w_qkv = scatter_about(key_list[4], (N_REP, 3 * D // N_REP, D), D ** -0.5, 0.125, ((1, 4),))
    b_qkv = scatter_about(key_list[5], (3 * D,), 0.3, 3.0, (), jnp.float32)
    w_out = scatter_about(key_list[6], (N_REP, D // N_REP, D), (D // 64) ** -0.5, 1.0, ((1, 4),))
    norm2_gain = jnp.clip(1.0 + 0.1 * jax.random.normal(key_list[7], (D,), jnp.float32), 0.5, 1.5)
    norm2_bias = scatter_about(key_list[8], (D,), 0.3, 3.0, (), jnp.float32)
    w_gate_up = scatter_about(key_list[9], (N_REP, 2 * FF // N_REP, D), D ** -0.5, 0.125, ((1, 4),))
    w_down = scatter_about(key_list[10], (N_REP, D // N_REP, FF), (FF // 4) ** -0.5, 0.15625, ((1, 4),))
    cotangent = bell_draw_with(key_list[11], (TOKENS, D), 1.0, 6.0, ((0, 32),), (0, 1, 32, 2.75))
    return {"tokens": tokens, "lengths": lengths, "norm1_gain": norm1_gain, "norm1_bias": norm1_bias, "w_qkv": w_qkv, "b_qkv": b_qkv, "w_out": w_out, "norm2_gain": norm2_gain, "norm2_bias": norm2_bias, "w_gate_up": w_gate_up, "w_down": w_down, "cotangent": cotangent}


@jax.custom_vjp
def low(v):
    return lax.optimization_barrier(v.astype(jnp.bfloat16)).astype(jnp.float32)

@jax.custom_vjp
def low_back(v):
    return v

def low_keep(v):
    return (low(v), None)

def low_pass(kept, grad):
    return (grad,)

def back_keep(v):
    return (v, None)

def back_low(kept, grad):
    return (low(grad),)
low.defvjp(low_keep, low_pass)
low_back.defvjp(back_keep, back_low)
EPSILON = 1e-05
MASKED = -1e+30

def layer_norm(inputs, gain, shift):
    center = inputs - lax.optimization_barrier(jnp.mean(inputs, axis=-1, keepdims=True))
    scaled = center * lax.rsqrt(lax.optimization_barrier(jnp.mean(center * center, axis=-1, keepdims=True)) + EPSILON)
    return scaled * gain + shift

def rotary_tables(seq_len):
    half_rot = ROT // 2
    index = jnp.arange(half_rot, dtype=jnp.float32)
    freqs = jnp.power(10000.0, -2.0 * index / ROT)
    angles = jnp.arange(seq_len, dtype=jnp.float32)[:, None] * freqs[None, :]
    return (jnp.cos(angles), jnp.sin(angles))

def rotate(values, cos_table, sin_table):
    half_rot = ROT // 2
    lead_part = values[..., :half_rot]
    pair_part = values[..., half_rot:ROT]
    cos_b = cos_table[:, None, :]
    sin_b = sin_table[:, None, :]
    return jnp.concatenate([lead_part * cos_b - pair_part * sin_b, pair_part * cos_b + lead_part * sin_b, values[..., ROT:]], axis=-1)

def matmul_t(left, right):
    return jnp.einsum('nlr,cr->nlc', left, right, precision=lax.Precision.HIGHEST)

def forward(inputs, seq_lengths, norm1_gain, norm1_bias, mat_qkv, b_qkv, mat_out, norm2_gain, norm2_bias, mat_gu, mat_down):
    count, seq_len, width = inputs.shape
    head_count = width // HEAD
    positions = jnp.arange(seq_len, dtype=jnp.int32)
    valid = (positions[None, :] < seq_lengths[:, None]).astype(jnp.float32)
    causal = (positions[None, :] <= positions[:, None])[None]
    allowed = causal & (positions[None, None, :] < seq_lengths[:, None, None])
    cos_table, sin_table = rotary_tables(seq_len)
    normed1 = low(layer_norm(inputs, norm1_gain, norm1_bias))
    project = low_back(matmul_t(normed1, mat_qkv) + b_qkv)
    query = project[..., :width].reshape(count, seq_len, head_count, HEAD)
    key_part = project[..., width:2 * width].reshape(count, seq_len, head_count, HEAD)
    value_part = project[..., 2 * width:].reshape(count, seq_len, head_count, HEAD)
    query_rot = low(rotate(query, cos_table, sin_table))
    key_rot = low(rotate(key_part, cos_table, sin_table))
    value_b = low(value_part)
    scores = low_back(jnp.einsum('nihd,njhd->nhij', query_rot, key_rot, precision=lax.Precision.HIGHEST) * HEAD ** (-0.5))
    scores = jnp.where(allowed[:, None], scores, MASKED)
    expo = jnp.exp(scores)
    probs = expo / lax.optimization_barrier(jnp.sum(expo, axis=-1, keepdims=True))
    attended = jnp.einsum('nhij,njhd->nihd', low(probs), value_b, precision=lax.Precision.HIGHEST)
    attended = low_back(low(attended)).reshape(count, seq_len, width)
    hidden_res = inputs + low_back(matmul_t(attended, mat_out))
    normed2 = low(layer_norm(hidden_res, norm2_gain, norm2_bias))
    both = low_back(matmul_t(normed2, mat_gu))
    ff_width = mat_down.shape[1]
    activ = low(jax.nn.silu(both[..., :ff_width]) * both[..., ff_width:])
    branch = low_back(matmul_t(activ, mat_down))
    return valid[..., None] * (hidden_res + branch)

def reference(tokens, lengths, norm1_gain, norm1_bias, w_qkv, b_qkv, w_out, norm2_gain, norm2_bias, w_gate_up, w_down, cotangent):
    params = (norm1_gain, norm1_bias, w_qkv.astype(jnp.float32).reshape(3 * D, D), b_qkv, w_out.astype(jnp.float32).reshape(D, D), norm2_gain, norm2_bias, w_gate_up.astype(jnp.float32).reshape(2 * FF, D), w_down.astype(jnp.float32).reshape(D, FF))
    per_block = 4 if SEQS % 4 == 0 else 1
    blocks_in = tokens.astype(jnp.float32).reshape(SEQS // per_block, per_block, LEN, D)
    blocks_len = lengths.astype(jnp.int32).reshape(SEQS // per_block, per_block)
    blocks_cot = cotangent.astype(jnp.float32).reshape(SEQS // per_block, per_block, LEN, D)

    def one_block(totals, pieces):
        block_in, block_len, block_cot = pieces

        def run_block(inputs, *weights):
            return forward(inputs, block_len, *weights)
        result, pullback = jax.vjp(run_block, block_in, *params)
        grads = pullback(block_cot)
        totals = tuple((total + grad for total, grad in zip(totals, grads[1:])))
        return (totals, (result, grads[0]))
    zero_grads = tuple((jnp.zeros_like(param) for param in params))
    totals, (block_outs, block_grads) = lax.scan(one_block, zero_grads, (blocks_in, blocks_len, blocks_cot))
    mixed = block_outs.reshape(TOKENS, D)
    grad_tokens = block_grads.reshape(TOKENS, D)
    return (mixed, grad_tokens, totals[0], totals[1], totals[2].reshape(N_REP, 3 * D // N_REP, D), totals[3], totals[4].reshape(N_REP, D // N_REP, D), totals[5], totals[6], totals[7].reshape(N_REP, 2 * FF // N_REP, D), totals[8].reshape(N_REP, D // N_REP, FF))
```

```python
import functools
import jax
import jax.numpy as jnp
from jax import lax
from jax.experimental import pallas as pl
from jax.experimental.pallas import tpu as pltpu
from jax.sharding import PartitionSpec as P

HEAD = 64
ROT = 16
LANES = 128
EPSILON = 1e-05
MASKED = -1e30
F32 = jnp.float32
BF16 = jnp.bfloat16


def layer_norm(inputs, gain, shift):
    center = inputs - jnp.mean(inputs, axis=-1, keepdims=True)
    inv_scale = lax.rsqrt(jnp.mean(center * center, axis=-1, keepdims=True) + EPSILON)
    scaled = center * inv_scale
    return (scaled * gain + shift, scaled, inv_scale)


def norm_back(grad_in, scaled, inv_scale, gain):
    weighted = grad_in * gain
    centered = weighted - jnp.mean(weighted, axis=-1, keepdims=True)
    return inv_scale * (centered - scaled * jnp.mean(weighted * scaled, axis=-1, keepdims=True))


def rotary_lanes(seq_len):
    half = ROT // 2
    lane = jnp.arange(LANES, dtype=jnp.int32) % HEAD
    freqs = jnp.power(10000.0, -2.0 * (lane % half).astype(F32) / ROT)
    angles = jnp.arange(seq_len, dtype=F32)[:, None] * freqs[None, :]
    cos, sin = jnp.cos(angles), jnp.sin(angles)
    c = jnp.where(lane < ROT, cos, 1.0)
    s_lead = jnp.where(lane < half, -sin, 0.0)
    s_pair = jnp.where((lane >= half) & (lane < ROT), sin, 0.0)
    return c, s_lead, s_pair


def dot(left, right, dims):
    return lax.dot_general(left, right, ((dims[0], dims[1]), ((), ())), preferred_element_type=F32)


def mm_t(left, right):
    return dot(left, right, ((1,), (1,)))


def mm(left, right):
    return dot(left, right, ((1,), (0,)))


def mm_tn(left, right):
    return dot(left, right, ((0,), (0,)))


def turn(u, c, s_lead, s_pair, back):
    half = ROT // 2
    lead = pltpu.roll(u, LANES - half, 1)
    pair = pltpu.roll(u, half, 1)
    if back:
        return u * c - lead * s_lead - pair * s_pair
    return u * c + lead * s_lead + pair * s_pair


def pair_probs(length, q2, k2, first):
    rows = q2.shape[0]
    zero = jnp.zeros_like(q2)
    stacked = jnp.concatenate([jnp.where(first, q2, zero), jnp.where(first, zero, q2)], axis=0)
    raw = mm_t(stacked, k2) * (HEAD ** (-0.5))
    i = lax.broadcasted_iota(jnp.int32, raw.shape, 0) % rows
    j = lax.broadcasted_iota(jnp.int32, raw.shape, 1)
    raw = jnp.where((j <= i) & (j < length), raw, MASKED)
    raw = raw - jnp.max(raw, axis=-1, keepdims=True)
    expo = jnp.exp(raw)
    return expo / jnp.sum(expo, axis=-1, keepdims=True)


def attn_fwd_kernel(len_ref, c_ref, sl_ref, sp_ref, q_ref, k_ref, v_ref, o_ref):
    tables = (c_ref[...], sl_ref[...], sp_ref[...])
    rows = q_ref.shape[0]
    q2 = turn(q_ref[...].astype(F32), *tables, False).astype(BF16)
    k2 = turn(k_ref[...].astype(F32), *tables, False).astype(BF16)
    first = lax.broadcasted_iota(jnp.int32, q2.shape, 1) < HEAD
    probs = pair_probs(len_ref[0], q2, k2, first).astype(BF16)
    out = mm(probs, v_ref[...])
    o_ref[...] = jnp.where(first, out[:rows], out[rows:]).astype(BF16)


def attn_bwd_kernel(len_ref, c_ref, sl_ref, sp_ref, q_ref, k_ref, v_ref, g_ref, dq_ref, dk_ref, dv_ref):
    tables = (c_ref[...], sl_ref[...], sp_ref[...])
    rows = q_ref.shape[0]
    scale = HEAD ** (-0.5)
    q2 = turn(q_ref[...].astype(F32), *tables, False).astype(BF16)
    k2 = turn(k_ref[...].astype(F32), *tables, False).astype(BF16)
    v2 = v_ref[...]
    g2 = g_ref[...]
    first = lax.broadcasted_iota(jnp.int32, q2.shape, 1) < HEAD
    probs = pair_probs(len_ref[0], q2, k2, first)
    probs_b = probs.astype(BF16)
    zero = jnp.zeros_like(g2)
    stacked = jnp.concatenate([jnp.where(first, g2, zero), jnp.where(first, zero, g2)], axis=0)
    grad_probs = mm_t(stacked, v2)
    delta = jnp.sum(probs * grad_probs, axis=-1, keepdims=True)
    grad_scores = (probs * (grad_probs - delta)).astype(BF16)
    dq = mm(grad_scores, k2)
    dq = jnp.where(first, dq[:rows], dq[rows:]) * scale
    dk = jnp.where(first, mm_tn(grad_scores[:rows], q2), mm_tn(grad_scores[rows:], q2)) * scale
    dv = jnp.where(first, mm_tn(probs_b[:rows], g2), mm_tn(probs_b[rows:], g2))
    dq_ref[...] = turn(dq, *tables, True).astype(BF16)
    dk_ref[...] = turn(dk, *tables, True).astype(BF16)
    dv_ref[...] = dv.astype(BF16)


def head_spec(seq_len, per_block, offset):
    return pl.BlockSpec(
        (None, seq_len, LANES), lambda p: ((p + offset) // per_block, 0, (p + offset) % per_block)
    )


def attention(lengths, tables, qkv_blocks, width):
    blocks, seq_len, cols = qkv_blocks.shape
    per_block = cols // LANES
    pairs = width // LANES
    table_spec = pl.BlockSpec((seq_len, LANES), lambda p: (0, 0))
    return pl.pallas_call(
        attn_fwd_kernel,
        grid=(pairs,),
        in_specs=[pl.BlockSpec(memory_space=pltpu.SMEM)]
        + [table_spec] * 3
        + [head_spec(seq_len, per_block, part * pairs) for part in range(3)],
        out_specs=pl.BlockSpec((seq_len, LANES), lambda p: (0, p)),
        out_shape=jax.ShapeDtypeStruct((seq_len, width), BF16),
        name="attn_fwd",
    )(lengths, *tables, qkv_blocks, qkv_blocks, qkv_blocks)


def attention_back(lengths, tables, qkv_blocks, grad_heads):
    blocks, seq_len, cols = qkv_blocks.shape
    width = grad_heads.shape[1]
    per_block = cols // LANES
    pairs = width // LANES
    table_spec = pl.BlockSpec((seq_len, LANES), lambda p: (0, 0))
    flat = pl.BlockSpec((seq_len, LANES), lambda p: (0, p))
    return pl.pallas_call(
        attn_bwd_kernel,
        grid=(pairs,),
        in_specs=[pl.BlockSpec(memory_space=pltpu.SMEM)]
        + [table_spec] * 3
        + [head_spec(seq_len, per_block, part * pairs) for part in range(3)]
        + [flat],
        out_specs=[flat] * 3,
        out_shape=[jax.ShapeDtypeStruct((seq_len, width), BF16)] * 3,
        name="attn_bwd",
    )(lengths, *tables, qkv_blocks, qkv_blocks, qkv_blocks, grad_heads)


def gather(value, axis):
    return lax.all_gather(value, axis, axis=0, tiled=True)


def scatter_sum(value, axis):
    return lax.psum_scatter(value, axis, scatter_dimension=0, tiled=True)


def body(
    tokens,
    lengths,
    norm1_gain,
    norm1_bias,
    w_qkv,
    b_qkv,
    w_out,
    norm2_gain,
    norm2_bias,
    w_gate_up,
    w_down,
    cotangent,
):
    seq_len, width = tokens.shape
    n_rep = lax.axis_size("rep")
    n_shard = lax.axis_size("shard")
    rep = lax.axis_index("rep")
    ff_width = w_down.shape[2]
    ff_own = ff_width // n_shard
    gate_blocks = n_rep // 2
    sub = w_gate_up.shape[1]
    qkv_cols = 3 * width // n_rep
    out_cols = width // n_rep
    positions = jnp.arange(seq_len, dtype=jnp.int32)
    valid = (positions < lengths[0]).astype(F32)[:, None]
    tables = rotary_lanes(seq_len)

    def own_block(weight):
        return lax.dynamic_index_in_dim(weight, rep, 0, keepdims=False)

    wq_block = gather(own_block(w_qkv), "shard")
    wo_full = gather(own_block(w_out), ("rep", "shard"))
    wd_block = own_block(w_down)
    wd_block = wd_block.reshape(-1, gate_blocks, n_shard, sub).transpose(2, 0, 1, 3)
    wd_block = lax.all_to_all(wd_block.reshape(n_shard, -1, ff_own), "shard", 0, 0)
    wd_own = gather(wd_block.reshape(out_cols, ff_own), "rep")
    wgu_own = w_gate_up.reshape(-1, width)

    grad_out = cotangent.astype(F32) * valid
    grad_out_b = grad_out.astype(BF16)
    dy_line = gather(grad_out_b, "shard")

    inputs = tokens.astype(F32)
    normed1, scaled1, inv1 = layer_norm(inputs, norm1_gain, norm1_bias)
    n1_plane = gather(normed1.astype(BF16), "rep")
    bias_block = lax.dynamic_slice_in_dim(b_qkv, rep * qkv_cols, qkv_cols)
    project = (mm_t(n1_plane, wq_block) + bias_block).astype(BF16)
    qkv_blocks = lax.all_to_all(project.reshape(n_rep, seq_len, qkv_cols), "rep", 0, 0)
    attended_b = attention(lengths, tables, qkv_blocks, width)
    hidden_res = inputs + mm_t(attended_b, wo_full)
    ob_plane = gather(attended_b, "rep")

    normed2, scaled2, inv2 = layer_norm(hidden_res, norm2_gain, norm2_bias)
    n2_line = gather(normed2.astype(BF16), "shard")
    both = mm_t(n2_line, wgu_own)
    gate_pre = both[:, :ff_own]
    up_pre = both[:, ff_own:]
    sigma = jax.nn.sigmoid(gate_pre)
    activ_b = (gate_pre * sigma * up_pre).astype(BF16)
    grad_activ = mm(dy_line, wd_own)
    grad_gate = grad_activ * up_pre * sigma * (1.0 + gate_pre * (1.0 - sigma))
    grad_up = grad_activ * gate_pre * sigma
    grad_both_b = jnp.concatenate([grad_gate, grad_up], axis=1).astype(BF16)
    dc_part = mm(grad_both_b, wgu_own).astype(BF16)
    grad_norm2_in = scatter_sum(dc_part, "shard").astype(F32)
    down_part = mm_t(activ_b, wd_own).astype(BF16)
    mixed = valid * (hidden_res + scatter_sum(down_part, "shard").astype(F32))

    gu_part = mm_tn(grad_both_b, n2_line).astype(BF16)
    owner_gu = lax.psum(gu_part, "rep").astype(F32).reshape(w_gate_up.shape)
    down_grad = mm_tn(dy_line, activ_b).astype(BF16)
    down_grad = scatter_sum(down_grad, "rep").reshape(n_shard, -1, ff_own)
    down_grad = lax.all_to_all(down_grad, "shard", 0, 0)
    down_grad = down_grad.reshape(n_shard, -1, gate_blocks, sub).transpose(1, 2, 0, 3)
    owner_down = gather(down_grad.reshape(1, -1, ff_width), "rep").astype(F32)

    gain2_grad = jnp.sum(grad_norm2_in * scaled2, axis=0)
    bias2_grad = jnp.sum(grad_norm2_in, axis=0)
    grad_hidden = grad_out + norm_back(grad_norm2_in, scaled2, inv2, norm2_gain)
    grad_attn_b = grad_hidden.astype(BF16)
    grad_heads_b = mm(grad_attn_b, wo_full).astype(BF16)
    grad_project_b = jnp.concatenate(
        attention_back(lengths, tables, qkv_blocks, grad_heads_b), axis=1
    )
    bias_qkv_grad = jnp.sum(grad_project_b.astype(F32), axis=0)
    dqkv_blocks = grad_project_b.reshape(seq_len, n_rep, qkv_cols).transpose(1, 0, 2)
    dqkv_plane = lax.all_to_all(dqkv_blocks, "rep", 0, 0).reshape(-1, qkv_cols)
    datt_blocks = grad_attn_b.reshape(seq_len, n_rep, out_cols).transpose(1, 0, 2)
    datt_plane = lax.all_to_all(datt_blocks, "rep", 0, 0).reshape(-1, out_cols)
    da_part = mm(dqkv_plane, wq_block).astype(BF16)
    grad_norm1_in = scatter_sum(da_part, "rep").astype(F32)
    gain1_grad = jnp.sum(grad_norm1_in * scaled1, axis=0)
    bias1_grad = jnp.sum(grad_norm1_in, axis=0)
    grad_tokens = grad_hidden + norm_back(grad_norm1_in, scaled1, inv1, norm1_gain)

    qkv_part = mm_tn(dqkv_plane, n1_plane).astype(BF16)
    out_part = mm_tn(datt_plane, ob_plane).astype(BF16)
    owner_qkv = gather(scatter_sum(qkv_part, "shard")[None], "rep").astype(F32)
    owner_out = gather(scatter_sum(out_part, "shard")[None], "rep").astype(F32)

    gain1_grad, bias1_grad, bias_qkv_grad, gain2_grad, bias2_grad = lax.psum(
        (gain1_grad, bias1_grad, bias_qkv_grad, gain2_grad, bias2_grad), ("rep", "shard")
    )
    return (
        mixed,
        grad_tokens,
        gain1_grad,
        bias1_grad,
        owner_qkv,
        bias_qkv_grad,
        owner_out,
        gain2_grad,
        bias2_grad,
        owner_gu,
        owner_down,
    )


def solution(mesh):
    tokens = P(("rep", "shard"), None)
    weight = P(None, "shard", None)
    return jax.shard_map(
        body,
        mesh=mesh,
        in_specs=(tokens, P(("rep", "shard")), P(), P(), weight, P(), weight, P(), P(), weight, weight, tokens),
        out_specs=(tokens, tokens, P(), P(), weight, P(), weight, P(), P(), weight, weight),
        check_vma=False,
    )
```
